256 devices in a mesh: sector: 32 (over x, z), chan: 8 (over y, core).
Axes of the slice: x: 4, y: 4, z: 8, core: 2. Of those that a mesh axis runs over, the one named last changes fastest.
Arguments:
- environment: bfloat16 [4096, 16, 640], P('sector', 'chan'), may hold values from -6 to 6
- sector_sizes: int32 [16], replicated, may hold values from 128 to 640, as said below
- joining_table: int32 [2, 2, 16], replicated, may hold values from 0 to 15, as said below
- isometry: bfloat16 [2, 2, 640, 4096], P(None, None, None, 'sector'), may hold values from -1 to 1
- mixing: float32 [2, 2, 16, 16], replicated, may hold values from -1 to 1
Outputs:
- environment_out: bfloat16 [4096, 16, 640], P('sector', 'chan')
The draws below stay inside these ranges and needn't reach their ends.
Inputs may be any that keep to these rules, and one draw needn't show every extreme that they name: `sector_sizes`: each a multiple of 128, of 1 to 5 tiles, all together 4096. `joining_table`: for every site step and site state a permutation of the 16 sectors that moves no sector by more than one place.
All inputs are finite; a program needn't handle non-finite values.
Results may differ from the reference program's by a relative error of at most 0.0065.
Values may be sent and summed in bfloat16 or wider, within the bound.
No kernel may reach another device: no remote copies, remote signals or barrier semaphores. Data moves between devices by JAX's collectives and lax.ppermute only.
A program may use at most 128 MiB of HBM per device.

```python
import jax
import jax.numpy as jnp
from jax import lax

BOND = 4096
TILE = 128
NSEC = 16
MAXK = 5
CH = 16
SITES = 2
W = 640


def sector_layout(key):
    base_key = jax.random.fold_in(key, 4711)
    all_tiles = BOND // TILE
    front_tiles = all_tiles // 2 - 2
    back_tiles = all_tiles - front_tiles - 2 * MAXK
    lowest = max(-(-front_tiles // MAXK), NSEC - 2 - back_tiles, 0)
    highest = min(((NSEC - 2) * MAXK - back_tiles) // MAXK, front_tiles, NSEC - 2)
    paired = jax.random.randint(jax.random.fold_in(base_key, 1), (), lowest, highest + 1).astype(jnp.int32)
    front_extra = front_tiles - paired
    back_extra = back_tiles - (NSEC - 2 - paired)
    free_slots = (NSEC - 2) * (MAXK - 1)
    shuffled = jax.random.permutation(jax.random.fold_in(base_key, 2), free_slots)
    slot_other = (shuffled // (MAXK - 1)).astype(jnp.int32)
    in_front = slot_other < paired
    in_back = jnp.logical_not(in_front)
    front_rank = jnp.cumsum(in_front.astype(jnp.int32)) - 1
    back_rank = jnp.cumsum(in_back.astype(jnp.int32)) - 1
    chosen = in_front & (front_rank < front_extra) | in_back & (back_rank < back_extra)
    others = jnp.arange(NSEC - 2, dtype=jnp.int32)
    counts = jnp.sum((chosen[:, None] & (slot_other[:, None] == others[None, :])).astype(jnp.int32), axis=0)
    sector_ids = jnp.where(others < paired, others, others + 2)
    sectors = jnp.arange(NSEC, dtype=jnp.int32)
    tile_counts = 1 + jnp.sum(jnp.where(sector_ids[:, None] == sectors[None, :], counts[:, None], 0), axis=0)
    tile_counts = jnp.where((sectors == paired) | (sectors == paired + 1), MAXK, tile_counts)
    return (tile_counts.astype(jnp.int32), paired)


def draw_sector_sizes(key, part):
    tile_counts, paired = sector_layout(key)
    return (tile_counts * TILE).astype(jnp.int32)


def settle(previous, flip_bit):
    chosen_swap = flip_bit * (1 - previous)
    return (chosen_swap, chosen_swap)


def draw_joining_table(key, part):
    tile_counts, paired = sector_layout(key)
    flip_bits = jax.random.randint(jax.random.fold_in(key, 5309), (SITES, 2, NSEC - 1), 0, 2).astype(jnp.int32)
    link_ids = jnp.arange(NSEC - 1, dtype=jnp.int32)
    second_state = (jnp.arange(2) == 1)[None, :, None]
    forced_on = (link_ids == paired)[None, None, :] & second_state
    forced_off = ((link_ids == paired - 1) | (link_ids == paired + 1))[None, None, :] & second_state
    flip_bits = jnp.where(forced_on, 1, jnp.where(forced_off, 0, flip_bits)).astype(jnp.int32)
    final_state, swap_bits = lax.scan(settle, jnp.zeros((SITES, 2), jnp.int32), jnp.moveaxis(flip_bits, 2, 0))
    swap_bits = jnp.moveaxis(swap_bits, 0, 2)
    edge = jnp.zeros((SITES, 2, 1), jnp.int32)
    raise_sector = jnp.concatenate([swap_bits, edge], axis=2)
    lower_sector = jnp.concatenate([edge, swap_bits], axis=2)
    permuted = jnp.arange(NSEC, dtype=jnp.int32)[None, None, :] + raise_sector - lower_sector
    return permuted.astype(jnp.int32)


def steps_of(stream_key, extent, split, low, largest):
    loudness, own = 1.0, jax.random.fold_in(stream_key, 6)
    for dim, parts in split:
        steps = jnp.exp(jax.random.uniform(jax.random.fold_in(own, dim), (parts,), jnp.float32, low / len(split), largest / len(split)))
        loudness = loudness * jnp.repeat(steps, extent[dim] // parts).reshape([-1 if axis == dim else 1 for axis in range(len(extent))])
    return loudness


def noise(own_key, shape, width, limit, shards=(), held_as=jnp.bfloat16):
    gain = steps_of(own_key, shape, shards, -0.22, 0.18) if shards else 1.0
    drawn = jax.random.normal(own_key, shape, jnp.float32) * width * gain
    return jnp.minimum(jnp.maximum(drawn, -limit), limit).astype(held_as)


def setup_inputs(seed: int = 0) -> dict:
    streams_of = jax.random.split(jax.random.key(seed), 6)
    return {
        "environment": noise(streams_of[0], (BOND, CH, W), 1.0, 6.0, ((0, 32), (1, 8))),
        "sector_sizes": draw_sector_sizes(jax.random.fold_in(streams_of[5], 71), 0),
        "joining_table": draw_joining_table(jax.random.fold_in(streams_of[5], 71), 0),
        "isometry": jnp.clip(jax.random.uniform(streams_of[3], (SITES, 2, W, BOND), jnp.float32, -1.0, 1.0) * steps_of(streams_of[3], (SITES, 2, W, BOND), ((3, 32),), -0.4, 0.0), -1.0, 1.0).astype(jnp.bfloat16),
        "mixing": noise(streams_of[4], (SITES, 2, CH, CH), (2 * CH) ** -0.5, 1.0, (), jnp.float32),
    }


def sector_starts(sector_sizes):
    tile_counts = sector_sizes // TILE
    tile_starts = jnp.cumsum(tile_counts) - tile_counts
    return (tile_starts * TILE).astype(jnp.int32)


def reference(environment, sector_sizes, joining_table, isometry, mixing):
    state_starts = sector_starts(sector_sizes)
    states = jnp.arange(BOND, dtype=jnp.int32)
    state_sector = (jnp.sum((states[:, None] >= state_starts[None, :]).astype(jnp.int32), axis=1) - 1).astype(jnp.int32)
    sector_ids = jnp.arange(NSEC, dtype=jnp.int32)
    row_width = jnp.sum(jnp.where(state_sector[:, None] == sector_ids[None, :], sector_sizes[None, :], 0), axis=1)
    column = jnp.arange(W, dtype=jnp.int32)
    current = environment
    for k in range(SITES):
        masked = jnp.where(column[None, None, :] < row_width[:, None, None], current, jnp.zeros((), jnp.bfloat16))
        padded = jnp.concatenate([masked, jnp.zeros((W, CH, W), jnp.bfloat16)], axis=0)
        map_columns = jnp.concatenate([isometry[k], jnp.zeros((2, W, W), jnp.bfloat16)], axis=2)
        anchors = jnp.argmax(joining_table[k][:, None, :] == sector_ids[None, :, None], axis=2).astype(jnp.int32)
        coefficients = mixing[k]

        def one_sector(building, target):
            summed = jnp.zeros((W, CH, W), jnp.float32)
            width_target = sector_sizes[target]
            for s in range(2):
                anchor = anchors[s, target]
                width_anchor = sector_sizes[anchor]
                source = lax.dynamic_slice_in_dim(padded, state_starts[anchor], W, 0)
                source = jnp.where((column < width_anchor)[:, None, None], source, jnp.zeros((), jnp.bfloat16))
                block_map = lax.dynamic_slice_in_dim(map_columns[s], state_starts[target], W, 1)
                keep_mask = (column < width_anchor)[:, None] & (column < width_target)[None, :]
                block_map = jnp.where(keep_mask, block_map, jnp.zeros((), jnp.bfloat16))
                contracted = jnp.einsum("ab,acj->bcj", block_map.astype(jnp.float32), source.astype(jnp.float32)).astype(jnp.bfloat16)
                sandwich = jnp.einsum("bcj,jd->bcd", contracted.astype(jnp.float32), block_map.astype(jnp.float32))
                sandwich = sandwich * (3.0 / width_anchor.astype(jnp.float32))
                summed = summed + jnp.einsum("bcd,cv->bvd", sandwich, coefficients[s], precision=lax.Precision.HIGHEST)
            updated = summed.astype(jnp.bfloat16)
            previous = lax.dynamic_slice_in_dim(building, state_starts[target], W, 0)
            updated = jnp.where((column < width_target)[:, None, None], updated, previous)
            return lax.dynamic_update_slice_in_dim(building, updated, state_starts[target], 0), None

        building = jnp.zeros((BOND + W, CH, W), jnp.bfloat16)
        building, unused_out = lax.scan(one_sector, building, sector_ids)
        current = building[:BOND]
    return current
```

```python
import jax
import jax.numpy as jnp
from jax import lax
from jax.sharding import PartitionSpec as P

TILE = 128
NSEC = 16
MAXK = 5
CHANS = 8
SPAN = 2 * MAXK - 1
BF16 = jnp.bfloat16
F32 = jnp.float32


def shifted(value, steps):
    count = lax.axis_size("sector")
    pairs = [(i, i - steps) for i in range(count) if 0 <= i - steps < count]
    return lax.ppermute(value, "sector", pairs)


def pick(table, position):
    ids = jnp.arange(table.shape[-1], dtype=jnp.int32)
    return jnp.sum(jnp.where(ids == position, table, 0), axis=-1)


def layout_tables(sector_sizes, joining_table, tiles):
    counts = sector_sizes // TILE
    ids = jnp.arange(NSEC, dtype=jnp.int32)
    starts = jnp.sum(jnp.where(ids[None, :] < ids[:, None], counts[None, :], 0), axis=1)
    tile = jnp.arange(tiles, dtype=jnp.int32)
    member = (tile[:, None] >= starts[None, :]) & (tile[:, None] < (starts + counts)[None, :])

    def by_tile(per_sector):
        return jnp.sum(jnp.where(member, per_sector[..., None, :], 0), axis=-1)

    own_start = by_tile(starts)
    own_count = by_tile(counts)
    joined = joining_table[..., None] == ids
    target_start = jnp.sum(jnp.where(joined, starts, 0), axis=-1)
    anchor_start = jnp.sum(jnp.where(joined, starts[:, None], 0), axis=-2)
    anchor_count = jnp.sum(jnp.where(joined, counts[:, None], 0), axis=-2)
    return own_start, own_count, by_tile(target_start), by_tile(anchor_start), by_tile(anchor_count)


def selection(own_start, anchor_start, anchor_count, tiles):
    slot = jnp.arange(MAXK, dtype=jnp.int32)
    tile = jnp.arange(tiles, dtype=jnp.int32)
    wanted = anchor_start[:, :, None] + slot
    valid = slot < anchor_count[:, :, None]
    source = (wanted[..., None] == tile) & valid[..., None]
    block = (tile - own_start)[:, None] == slot
    return (source[..., None] & block[None, :, None, None, :]).astype(BF16)


def exchange(blocks, chosen, tiles):
    spread = lax.all_to_all(blocks, ("sector", "chan"), 0, 0, tiled=True)
    spread = spread.reshape(tiles, CHANS, 2, MAXK, TILE)
    routed = jnp.einsum(
        "snitj,tcsja->nsica", chosen, spread, preferred_element_type=F32
    ).astype(BF16)
    routed = routed.reshape(tiles, 2 * MAXK * CHANS, TILE)
    landed = lax.all_to_all(routed, "sector", 0, 0, tiled=True)
    return landed.reshape(tiles, 2, MAXK, CHANS, TILE)


def per_device(environment, sector_sizes, joining_table, isometry, mixing):
    tiles = lax.axis_size("sector")
    position = lax.axis_index("sector")
    chan = lax.axis_index("chan")
    window = environment.shape[2]
    part = window // CHANS
    fine = TILE // CHANS

    slices = lax.dynamic_slice_in_dim(isometry, chan * part, part, 2)
    own_start, own_count, target_start, anchor_start, anchor_count = layout_tables(
        sector_sizes, joining_table, tiles
    )
    my_start = pick(own_start, position)
    my_width = pick(own_count, position) * TILE
    my_target = pick(target_start, position)
    my_anchor_width = pick(anchor_count, position) * TILE

    maps = []
    for k in range(2):
        near = [slices[k] if d == 0 else shifted(slices[k], d) for d in range(-SPAN, SPAN + 1)]
        near = jnp.stack(near)
        own = lax.dynamic_slice_in_dim(near, my_start - position + SPAN, MAXK, 0)
        outs = [
            lax.dynamic_slice_in_dim(near[:, s], my_target[k, s] - position + SPAN, MAXK, 0)
            for s in range(2)
        ]
        chosen = jnp.stack([own[:, 0], own[:, 1], outs[0], outs[1]])
        full = lax.all_gather(chosen, "chan", axis=0)
        full = full.transpose(1, 0, 3, 2, 4).reshape(4, window, window)
        maps.append((full[:2], full[2:]))
    (own0, out0), (own1, out1) = maps

    column = jnp.arange(window, dtype=jnp.int32)
    masked = jnp.where(column < my_width, environment, jnp.zeros((), BF16))

    first = jnp.einsum("sjd,awj->sdwa", out0, masked, preferred_element_type=F32).astype(BF16)
    first = first.reshape(2, MAXK, CHANS, fine, 2, TILE).transpose(3, 4, 2, 0, 1, 5)
    first = first.reshape(tiles * CHANS, 2 * MAXK, TILE)
    select0 = selection(own_start, anchor_start[0], anchor_count[0], tiles)
    landed = exchange(first, select0, tiles)
    rows = landed.transpose(1, 0, 3, 2, 4).reshape(2, tiles * CHANS, window)
    second = jnp.einsum("sra,sab->srb", rows, own0, preferred_element_type=F32)
    same = jnp.eye(fine, dtype=F32)
    scale0 = 3.0 / my_anchor_width[0].astype(F32)
    weights0 = (mixing[0] * scale0[:, None, None]).reshape(2, CHANS, 2, 2 * CHANS)
    blend0 = jnp.einsum("de,scwv->dvsewc", same, weights0).reshape(fine * 2 * CHANS, -1)
    mixed = jnp.dot(blend0, second.reshape(-1, window), precision=lax.Precision.HIGHEST)
    middle = jnp.where(column < my_width, mixed, 0.0).astype(BF16)

    third = jnp.einsum("ra,sab->srb", middle, out1, preferred_element_type=F32)
    scale1 = 3.0 / my_width.astype(F32)
    weights1 = (mixing[1] * scale1).reshape(2, 2 * CHANS, CHANS, 2)
    blend1 = jnp.einsum("je,swcv->sjvcew", same, weights1).reshape(2, tiles * CHANS, -1)
    fourth = jnp.einsum("spr,srb->psb", blend1, third, precision=lax.Precision.HIGHEST).astype(BF16)
    fourth = fourth.reshape(tiles * CHANS, 2 * MAXK, TILE)
    select1 = selection(own_start, anchor_start[1], anchor_count[1], tiles)
    landed = exchange(fourth, select1, tiles)
    landed = landed.reshape(fine, 2, 2, MAXK, CHANS, TILE)
    result = jnp.einsum(
        "jvsicb,sicjd->bvd",
        landed,
        own1.reshape(2, MAXK, CHANS, fine, window),
        preferred_element_type=F32,
    )
    return jnp.where(column < my_width, result, 0.0).astype(BF16)


def solution(mesh):
    placed = (P("sector", "chan", None), P(), P(), P(None, None, None, "sector"), P())
    return jax.shard_map(
        per_device, mesh=mesh, in_specs=placed, out_specs=P("sector", "chan", None), check_vma=False
    )
```

```python
import jax
import jax.numpy as jnp
from jax import lax
from jax.sharding import PartitionSpec as P

TILE = 128
NSEC = 16
MAXK = 5
CHANS = 8
BF16 = jnp.bfloat16
F32 = jnp.float32


def pick(table, position):
    ids = jnp.arange(table.shape[-1], dtype=jnp.int32)
    return jnp.sum(jnp.where(ids == position, table, 0), axis=-1)


def layout_tables(sector_sizes, joining_table, tiles):
    counts = sector_sizes // TILE
    ids = jnp.arange(NSEC, dtype=jnp.int32)
    starts = jnp.sum(jnp.where(ids[None, :] < ids[:, None], counts[None, :], 0), axis=1)
    tile = jnp.arange(tiles, dtype=jnp.int32)
    member = (tile[:, None] >= starts[None, :]) & (tile[:, None] < (starts + counts)[None, :])
    joined = joining_table[..., None] == ids

    def by_tile(per_sector):
        return jnp.sum(jnp.where(member, per_sector[..., None, :], 0), axis=-1)

    def both(select):
        return by_tile(select(starts)), by_tile(select(counts))

    own = both(lambda v: v)
    target = both(lambda v: jnp.sum(jnp.where(joined, v, 0), axis=-1))
    anchor = both(lambda v: jnp.sum(jnp.where(joined, v[:, None], 0), axis=-2))
    return own, target, anchor


def sources(start, count, tiles):
    slot = jnp.arange(MAXK, dtype=jnp.int32)
    tile = jnp.arange(tiles, dtype=jnp.int32)
    wanted = jnp.where(slot < count[..., None], start[..., None] + slot, -1)
    return wanted[..., None] == tile


def selection(own_start, anchor, tiles):
    slot = jnp.arange(MAXK, dtype=jnp.int32)
    tile = jnp.arange(tiles, dtype=jnp.int32)
    block = (tile - own_start)[:, None] == slot
    return (sources(*anchor, tiles)[..., None] & block[None, :, None, None, :]).astype(BF16)


def route(chosen, spread):
    return jnp.einsum("snitj,tsjca->nsica", chosen, spread, preferred_element_type=F32).astype(BF16)


def deliver(blocks):
    return lax.all_to_all(blocks, "sector", 0, 0, tiled=True)


def per_device(environment, sector_sizes, joining_table, isometry, mixing):
    tiles = lax.axis_size("sector")
    position = lax.axis_index("sector")
    chan = lax.axis_index("chan")
    window = environment.shape[2]
    part = window // CHANS
    fine = TILE // CHANS
    piece = -(-part // tiles)

    own, target, anchor = layout_tables(sector_sizes, joining_table, tiles)
    width = pick(own[1], position) * TILE

    column = jnp.arange(window, dtype=jnp.int32)
    masked = jnp.where(column < width, environment, jnp.zeros((), BF16)).transpose(1, 0, 2)
    gathered = lax.all_gather(masked, "chan", axis=0, tiled=True)

    slim = lax.dynamic_slice_in_dim(isometry[0], chan * fine, fine, 2)
    slim = slim.transpose(0, 2, 1).reshape(2, part, TILE)
    slices = lax.dynamic_slice_in_dim(isometry, chan * part, part, 2)
    kinds = jnp.concatenate([slim[None], slices])
    kinds = jnp.pad(kinds, ((0, 0), (0, 0), (0, tiles * piece - part), (0, 0)))
    kinds = kinds.reshape(6, tiles, piece, TILE).transpose(1, 0, 2, 3)
    spread = deliver(kinds.reshape(tiles, 6 * piece, TILE)).reshape(tiles, 3, 2, piece, TILE)
    mine = jnp.broadcast_to(sources(*own, tiles), (2, tiles, MAXK, tiles)).astype(BF16)
    theirs = sources(*target, tiles).astype(BF16)
    picks = [(theirs[0], 0), (mine, 1), (theirs[1], 2), (mine, 2)]
    routed = [
        jnp.einsum("snit,tsrd->nsird", hot, spread[:, kind], preferred_element_type=F32)
        for hot, kind in picks
    ]
    routed = jnp.stack(routed, axis=1).astype(BF16)
    landed = deliver(routed.reshape(tiles, 8 * MAXK * piece, TILE))
    landed = landed.reshape(tiles, 4, 2 * MAXK, piece, TILE)

    def rows_of(groups):
        moved = groups.transpose(0, 3, 1, 2, 4)
        return moved.reshape(tiles * piece, -1)[:part]

    maps_a = lax.all_gather(rows_of(landed[:, 1:3]), "chan", axis=0, tiled=True)
    maps_b = lax.all_gather(rows_of(landed[:, 3:4]), "chan", axis=0, tiled=True)
    maps_a = maps_a.reshape(window, 2, 2, window)
    own0, out1 = maps_a[:, 0], maps_a[:, 1]
    slim = landed[:, 0].transpose(1, 0, 2, 3).reshape(2 * MAXK, tiles * piece, TILE)[:, :part]
    slim = slim.reshape(2 * MAXK * fine, window)

    first = jnp.einsum("dj,waj->wda", slim, gathered, preferred_element_type=F32).astype(BF16)
    first = first.reshape(2, CHANS, 2 * MAXK, fine, TILE).transpose(3, 0, 2, 1, 4)
    first = deliver(first.reshape(tiles, 2 * MAXK * CHANS, TILE))
    select0 = selection(own[0], (anchor[0][0], anchor[1][0]), tiles)
    first = route(select0, first.reshape(tiles, 2, MAXK, CHANS, TILE))
    first = deliver(first.reshape(tiles, 2 * MAXK * CHANS, TILE))
    rows = first.reshape(tiles, 2, MAXK, CHANS, TILE).transpose(1, 0, 3, 2, 4)
    rows = rows.reshape(2, tiles * CHANS, window)
    second = jnp.einsum("sra,asb->srb", rows, own0, preferred_element_type=F32)
    same = jnp.eye(fine, dtype=F32)
    scale0 = 3.0 / (pick(anchor[1][0], position) * TILE).astype(F32)
    weights0 = mixing[0] * scale0[:, None, None]
    blend0 = jnp.einsum("de,swv->dvsew", same, weights0).reshape(fine * 2 * CHANS, -1)
    mixed = jnp.dot(blend0, second.reshape(-1, window), precision=lax.Precision.HIGHEST)
    middle = mixed.astype(BF16)

    third = jnp.einsum("ra,asb->srb", middle, out1, preferred_element_type=F32)
    scale1 = 3.0 / width.astype(F32)
    weights1 = (mixing[1] * scale1).reshape(2, 2 * CHANS, CHANS, 2)
    blend1 = jnp.einsum("je,swcv->sjvcew", same, weights1).reshape(2, tiles * CHANS, -1)
    fourth = jnp.einsum("spr,srb->psb", blend1, third, precision=lax.Precision.HIGHEST).astype(BF16)
    fourth = fourth.reshape(tiles * CHANS, 2 * MAXK, TILE)
    fourth = lax.all_to_all(fourth, ("sector", "chan"), 0, 0, tiled=True)
    fourth = fourth.reshape(tiles, CHANS, 2, MAXK, TILE).transpose(0, 2, 3, 1, 4)
    select1 = selection(own[0], (anchor[0][1], anchor[1][1]), tiles)
    fourth = deliver(route(select1, fourth).reshape(tiles, 2 * MAXK * CHANS, TILE))
    result = jnp.einsum(
        "jvsicb,icjsd->bvd",
        fourth.reshape(fine, 2, 2, MAXK, CHANS, TILE),
        maps_b.reshape(MAXK, CHANS, fine, 2, window),
        preferred_element_type=F32,
    )
    return result.astype(BF16)


def solution(mesh):
    placed = (P("sector", "chan", None), P(), P(), P(None, None, None, "sector"), P())
    return jax.shard_map(
        per_device, mesh=mesh, in_specs=placed, out_specs=P("sector", "chan", None), check_vma=False
    )
```

```python
import jax
import jax.numpy as jnp
from jax import lax
from jax.sharding import PartitionSpec as P

TILE = 128
NSEC = 16
MAXK = 5
CHANS = 8
BF16 = jnp.bfloat16
F32 = jnp.float32


def pick(table, position):
    ids = jnp.arange(table.shape[-1], dtype=jnp.int32)
    return jnp.sum(jnp.where(ids == position, table, 0), axis=-1)


def layout_tables(sector_sizes, joining_table, tiles):
    counts = sector_sizes // TILE
    ids = jnp.arange(NSEC, dtype=jnp.int32)
    starts = jnp.sum(jnp.where(ids[None, :] < ids[:, None], counts[None, :], 0), axis=1)
    tile = jnp.arange(tiles, dtype=jnp.int32)
    member = (tile[:, None] >= starts[None, :]) & (tile[:, None] < (starts + counts)[None, :])
    joined = joining_table[..., None] == ids

    def by_tile(per_sector):
        return jnp.sum(jnp.where(member, per_sector[..., None, :], 0), axis=-1)

    def both(select):
        return by_tile(select(starts)), by_tile(select(counts))

    own = both(lambda v: v)
    target = both(lambda v: jnp.sum(jnp.where(joined, v, 0), axis=-1))
    anchor = both(lambda v: jnp.sum(jnp.where(joined, v[:, None], 0), axis=-2))
    return own, target, anchor


def sources(start, count, tiles):
    slot = jnp.arange(MAXK, dtype=jnp.int32)
    tile = jnp.arange(tiles, dtype=jnp.int32)
    wanted = jnp.where(slot < count[..., None], start[..., None] + slot, -1)
    return wanted[..., None] == tile


def selection(own_start, anchor, tiles):
    slot = jnp.arange(MAXK, dtype=jnp.int32)
    tile = jnp.arange(tiles, dtype=jnp.int32)
    block = (tile - own_start)[:, None] == slot
    return (sources(*anchor, tiles)[..., None] & block[None, :, None, None, :]).astype(BF16)


def route(chosen, spread):
    return jnp.einsum("snitj,tsjca->nsica", chosen, spread, preferred_element_type=F32).astype(BF16)


def deliver(blocks):
    return lax.all_to_all(blocks, "sector", 0, 0, tiled=True)


def per_device(environment, sector_sizes, joining_table, isometry, mixing):
    tiles = lax.axis_size("sector")
    position = lax.axis_index("sector")
    chan = lax.axis_index("chan")
    window = environment.shape[2]
    part = window // CHANS
    fine = TILE // CHANS
    half = tiles // 2
    piece = part // half
    exact = lax.Precision.HIGHEST

    gathered = lax.all_gather(environment.transpose(1, 0, 2), "chan", axis=0, tiled=True)

    slim = lax.dynamic_slice_in_dim(isometry[0], chan * fine, fine, 2)
    slim = slim.transpose(0, 2, 1).reshape(2, part, TILE)
    slices = lax.dynamic_slice_in_dim(isometry, chan * part, part, 2)
    kinds = jnp.concatenate([slim[None], slices])
    kinds = kinds.reshape(3, tiles, piece, TILE).transpose(1, 0, 2, 3)
    spread = deliver(kinds.reshape(tiles, 3 * piece, TILE)).reshape(tiles, 3, piece, TILE)

    own, target, anchor = layout_tables(sector_sizes, joining_table, tiles)
    width = pick(own[1], position) * TILE
    mine = sources(*own, tiles).astype(BF16)
    theirs = sources(*target, tiles).astype(BF16)
    theirs = jnp.where(position < half, theirs[:, 0], theirs[:, 1])
    picks = [(theirs[0], 0), (mine, 1), (theirs[1], 2), (mine, 2)]
    routed = [
        jnp.einsum("nit,trd->nird", hot, spread[:, kind], preferred_element_type=F32)
        for hot, kind in picks
    ]
    routed = jnp.stack(routed, axis=1).astype(BF16)
    landed = deliver(routed.reshape(tiles, 4 * MAXK * piece, TILE))
    landed = landed.reshape(2, half, 4, MAXK, piece, TILE)

    def rows_of(groups):
        return groups.transpose(1, 4, 2, 0, 3, 5).reshape(part, -1)

    maps_a = lax.all_gather(rows_of(landed[:, :, 1:3]), "chan", axis=0, tiled=True)
    maps_b = lax.all_gather(rows_of(landed[:, :, 3:4]), "chan", axis=0, tiled=True)
    slim = landed[:, :, 0].transpose(0, 2, 1, 3, 4).reshape(2 * MAXK * fine, window)
    column = jnp.arange(window, dtype=jnp.int32)
    slim = jnp.where(column < width, slim, jnp.zeros((), BF16))

    first = jnp.einsum("dj,waj->wda", slim, gathered, preferred_element_type=F32).astype(BF16)
    first = first.reshape(2, CHANS, 2 * MAXK, fine, TILE).transpose(3, 0, 2, 1, 4)
    first = deliver(first.reshape(tiles, 2 * MAXK * CHANS, TILE))
    select0 = selection(own[0], (anchor[0][0], anchor[1][0]), tiles)
    first = route(select0, first.reshape(tiles, 2, MAXK, CHANS, TILE))
    first = deliver(first.reshape(tiles, 2 * MAXK * CHANS, TILE))
    rows = first.reshape(tiles, 2, MAXK, CHANS, TILE).transpose(1, 0, 3, 2, 4)
    rows = rows.reshape(2, tiles * CHANS, window)

    row = jnp.arange(tiles * CHANS, dtype=jnp.int32)
    channel = jnp.arange(2 * CHANS, dtype=jnp.int32)
    natural = ((row % (2 * CHANS))[:, None] == channel).astype(F32)
    paired = 2 * (row % CHANS) + (row // CHANS) % 2
    paired = (paired[:, None] == channel).astype(F32)
    same = (row // (2 * CHANS))[:, None] == (row // (2 * CHANS))[None, :]

    def blend(coefficients, out_rows):
        spread_out = jnp.einsum("rv,wv->rw", out_rows, coefficients, precision=exact)
        spread_out = jnp.einsum("rw,qw->rq", spread_out, natural, precision=exact)
        return jnp.where(same, spread_out, 0.0)

    scale0 = 3.0 / (pick(anchor[1][0], position) * TILE).astype(F32)
    scale1 = 3.0 / width.astype(F32)
    mixed = jnp.zeros((tiles * CHANS, window), F32)
    for s in range(2):
        second = jnp.dot(
            rows[s], maps_a[:, s * window : (s + 1) * window], preferred_element_type=F32
        )
        mixed = mixed + jnp.dot(blend(mixing[0, s] * scale0[s], natural), second, precision=exact)
    middle = mixed.astype(BF16)

    fourth = []
    for s in range(2, 4):
        third = jnp.dot(
            middle, maps_a[:, s * window : (s + 1) * window], preferred_element_type=F32
        )
        fourth.append(jnp.dot(blend(mixing[1, s - 2] * scale1, paired), third, precision=exact))
    fourth = jnp.stack(fourth, axis=1).astype(BF16)
    fourth = lax.all_to_all(fourth, ("sector", "chan"), 0, 0, tiled=True)
    fourth = fourth.reshape(tiles, CHANS, 2, MAXK, TILE).transpose(0, 2, 3, 1, 4)
    select1 = selection(own[0], (anchor[0][1], anchor[1][1]), tiles)
    fourth = deliver(route(select1, fourth).reshape(tiles, 2 * MAXK * CHANS, TILE))
    result = jnp.einsum(
        "jvsicb,icjsd->bvd",
        fourth.reshape(fine, 2, 2, MAXK, CHANS, TILE),
        maps_b.reshape(MAXK, CHANS, fine, 2, window),
        preferred_element_type=F32,
    )
    return result.astype(BF16)


def solution(mesh):
    placed = (P("sector", "chan", None), P(), P(), P(None, None, None, "sector"), P())
    return jax.shard_map(
        per_device, mesh=mesh, in_specs=placed, out_specs=P("sector", "chan", None), check_vma=False
    )
```

```python
import jax
import jax.numpy as jnp
from jax import lax
from jax.sharding import PartitionSpec as P

TILE = 128
NSEC = 16
MAXK = 5
CHANS = 8
BF16 = jnp.bfloat16
F32 = jnp.float32


def pick(table, position):
    ids = jnp.arange(table.shape[-1], dtype=jnp.int32)
    return jnp.sum(jnp.where(ids == position, table, 0), axis=-1)


def layout_tables(sector_sizes, joining_table, tiles):
    counts = sector_sizes // TILE
    ids = jnp.arange(NSEC, dtype=jnp.int32)
    starts = jnp.sum(jnp.where(ids[None, :] < ids[:, None], counts[None, :], 0), axis=1)
    tile = jnp.arange(tiles, dtype=jnp.int32)
    member = (tile[:, None] >= starts[None, :]) & (tile[:, None] < (starts + counts)[None, :])
    joined = joining_table[..., None] == ids

    def by_tile(per_sector):
        return jnp.sum(jnp.where(member, per_sector[..., None, :], 0), axis=-1)

    def both(select):
        return by_tile(select(starts)), by_tile(select(counts))

    own = both(lambda v: v)
    target = both(lambda v: jnp.sum(jnp.where(joined, v, 0), axis=-1))
    anchor = both(lambda v: jnp.sum(jnp.where(joined, v[:, None], 0), axis=-2))
    return own, target, anchor


def sources(start, count, tiles):
    slot = jnp.arange(MAXK, dtype=jnp.int32)
    tile = jnp.arange(tiles, dtype=jnp.int32)
    wanted = jnp.where(slot < count[..., None], start[..., None] + slot, -1)
    return wanted[..., None] == tile


def selection(own_start, anchor, tiles):
    slot = jnp.arange(MAXK, dtype=jnp.int32)
    tile = jnp.arange(tiles, dtype=jnp.int32)
    block = (tile - own_start)[:, None] == slot
    return (sources(*anchor, tiles)[..., None] & block[None, :, None, None, :]).astype(BF16)


def route(chosen, spread):
    return jnp.einsum("snitj,tsjca->nsica", chosen, spread, preferred_element_type=F32).astype(BF16)


def deliver(blocks):
    return lax.all_to_all(blocks, "sector", 0, 0, tiled=True)


def per_device(environment, sector_sizes, joining_table, isometry, mixing):
    tiles = lax.axis_size("sector")
    position = lax.axis_index("sector")
    chan = lax.axis_index("chan")
    window = environment.shape[2]
    part = window // CHANS
    fine = TILE // CHANS
    half = tiles // 2
    piece = part // half
    exact, fast = lax.Precision.HIGHEST, lax.Precision.HIGH

    gathered = lax.all_gather(environment.transpose(1, 0, 2), "chan", axis=0, tiled=True)

    slim = lax.dynamic_slice_in_dim(isometry[0], chan * fine, fine, 2)
    slim = slim.transpose(0, 2, 1).reshape(2, part, TILE)
    slices = lax.dynamic_slice_in_dim(isometry, chan * part, part, 2)
    kinds = jnp.concatenate([slim[None], slices])
    kinds = kinds.reshape(3, tiles, piece, TILE).transpose(1, 0, 2, 3)
    spread = deliver(kinds.reshape(tiles, 3 * piece, TILE)).reshape(tiles, 3, piece, TILE)

    own, target, anchor = layout_tables(sector_sizes, joining_table, tiles)
    width = pick(own[1], position) * TILE
    anchor_width = pick(anchor[1][0], position) * TILE
    width, anchor_width, spread = lax.optimization_barrier((width, anchor_width, spread))
    mine = sources(*own, tiles).astype(BF16)
    theirs = sources(*target, tiles).astype(BF16)
    theirs = jnp.where(position < half, theirs[:, 0], theirs[:, 1])
    picks = [(theirs[0], 0), (mine, 1), (theirs[1], 2), (mine, 2)]
    routed = [
        jnp.einsum("nit,trd->nird", hot, spread[:, kind], preferred_element_type=F32)
        for hot, kind in picks
    ]
    routed = jnp.stack(routed, axis=1).astype(BF16)
    landed = deliver(routed.reshape(tiles, 4 * MAXK * piece, TILE))
    landed = landed.reshape(2, half, 4, MAXK, piece, TILE)

    def rows_of(groups):
        return groups.transpose(1, 4, 2, 0, 3, 5).reshape(part, -1)

    maps_a = lax.all_gather(rows_of(landed[:, :, 1:3]), "chan", axis=0, tiled=True)
    maps_b = lax.all_gather(rows_of(landed[:, :, 3:4]), "chan", axis=0, tiled=True)
    slim = landed[:, :, 0].transpose(0, 2, 1, 3, 4).reshape(2 * MAXK * fine, window)
    column = jnp.arange(window, dtype=jnp.int32)
    slim = jnp.where(column < width, slim, jnp.zeros((), BF16))

    first = jnp.einsum("dj,waj->wda", slim, gathered, preferred_element_type=F32).astype(BF16)
    first = first.reshape(2, CHANS, 2 * MAXK, fine, TILE).transpose(3, 0, 2, 1, 4)
    first = deliver(first.reshape(tiles, 2 * MAXK * CHANS, TILE))
    select0 = selection(own[0], (anchor[0][0], anchor[1][0]), tiles)
    first = route(select0, first.reshape(tiles, 2, MAXK, CHANS, TILE))
    first = deliver(first.reshape(tiles, 2 * MAXK * CHANS, TILE))
    rows = first.reshape(tiles, 2, MAXK, CHANS, TILE).transpose(1, 0, 3, 2, 4)
    rows = rows.reshape(2, tiles * CHANS, window)

    row = jnp.arange(tiles * CHANS, dtype=jnp.int32)
    channel = jnp.arange(2 * CHANS, dtype=jnp.int32)
    natural = ((row % (2 * CHANS))[:, None] == channel).astype(F32)
    paired = 2 * (row % CHANS) + (row // CHANS) % 2
    paired = (paired[:, None] == channel).astype(F32)
    same = (row // (2 * CHANS))[:, None] == (row // (2 * CHANS))[None, :]

    def blend(coefficients, out_rows):
        spread_out = jnp.einsum("rv,wv->rw", out_rows, coefficients, precision=exact)
        spread_out = jnp.einsum("rw,qw->rq", spread_out, natural, precision=exact)
        return jnp.where(same, spread_out, 0.0)

    scale0 = 3.0 / anchor_width.astype(F32)
    scale1 = 3.0 / width.astype(F32)
    mixed = jnp.zeros((tiles * CHANS, window), F32)
    for s in range(2):
        second = jnp.dot(
            rows[s], maps_a[:, s * window : (s + 1) * window], preferred_element_type=F32
        )
        mixed = mixed + jnp.dot(blend(mixing[0, s] * scale0[s], natural), second, precision=fast)
    middle = mixed.astype(BF16)

    fourth = []
    for s in range(2, 4):
        third = jnp.dot(
            middle, maps_a[:, s * window : (s + 1) * window], preferred_element_type=F32
        )
        fourth.append(jnp.dot(blend(mixing[1, s - 2] * scale1, paired), third, precision=fast))
    fourth = jnp.stack(fourth, axis=1).astype(BF16)
    fourth = lax.all_to_all(fourth, ("sector", "chan"), 0, 0, tiled=True)
    fourth = fourth.reshape(tiles, CHANS, 2, MAXK, TILE).transpose(0, 2, 3, 1, 4)
    select1 = selection(own[0], (anchor[0][1], anchor[1][1]), tiles)
    fourth = deliver(route(select1, fourth).reshape(tiles, 2 * MAXK * CHANS, TILE))
    result = jnp.einsum(
        "jvsicb,icjsd->bvd",
        fourth.reshape(fine, 2, 2, MAXK, CHANS, TILE),
        maps_b.reshape(MAXK, CHANS, fine, 2, window),
        preferred_element_type=F32,
    )
    return result.astype(BF16)


def solution(mesh):
    placed = (P("sector", "chan", None), P(), P(), P(None, None, None, "sector"), P())
    return jax.shard_map(
        per_device, mesh=mesh, in_specs=placed, out_specs=P("sector", "chan", None), check_vma=False
    )
```

```python
import jax
import jax.numpy as jnp
from jax import lax
from jax.sharding import PartitionSpec as P

TILE = 128
NSEC = 16
MAXK = 5
CHANS = 8
BF16 = jnp.bfloat16
F32 = jnp.float32


def pick(table, position):
    ids = jnp.arange(table.shape[-1], dtype=jnp.int32)
    return jnp.sum(jnp.where(ids == position, table, 0), axis=-1)


def layout_tables(sector_sizes, joining_table, tiles):
    counts = sector_sizes // TILE
    ids = jnp.arange(NSEC, dtype=jnp.int32)
    starts = jnp.sum(jnp.where(ids[None, :] < ids[:, None], counts[None, :], 0), axis=1)
    tile = jnp.arange(tiles, dtype=jnp.int32)
    member = (tile[:, None] >= starts[None, :]) & (tile[:, None] < (starts + counts)[None, :])
    joined = joining_table[..., None] == ids

    def by_tile(per_sector):
        return jnp.sum(jnp.where(member, per_sector[..., None, :], 0), axis=-1)

    def both(select):
        return by_tile(select(starts)), by_tile(select(counts))

    own = both(lambda v: v)
    target = both(lambda v: jnp.sum(jnp.where(joined, v, 0), axis=-1))
    anchor = both(lambda v: jnp.sum(jnp.where(joined, v[:, None], 0), axis=-2))
    return own, target, anchor


def sources(start, count, tiles):
    slot = jnp.arange(MAXK, dtype=jnp.int32)
    tile = jnp.arange(tiles, dtype=jnp.int32)
    wanted = jnp.where(slot < count[..., None], start[..., None] + slot, -1)
    return wanted[..., None] == tile


def selection(own_start, anchor, tiles):
    slot = jnp.arange(MAXK, dtype=jnp.int32)
    tile = jnp.arange(tiles, dtype=jnp.int32)
    block = (tile - own_start)[:, None] == slot
    return (sources(*anchor, tiles)[..., None] & block[None, :, None, None, :]).astype(BF16)


def route(chosen, spread):
    return jnp.einsum("snitj,tsjca->nsica", chosen, spread, preferred_element_type=F32).astype(BF16)


def deliver(blocks):
    return lax.all_to_all(blocks, "sector", 0, 0, tiled=True)


def per_device(environment, sector_sizes, joining_table, isometry, mixing):
    tiles = lax.axis_size("sector")
    position = lax.axis_index("sector")
    chan = lax.axis_index("chan")
    window = environment.shape[2]
    part = window // CHANS
    fine = TILE // CHANS
    half = tiles // 2
    piece = part // half
    exact, fast = lax.Precision.HIGHEST, lax.Precision.HIGH

    gathered = lax.all_gather(environment.transpose(1, 0, 2), "chan", axis=0, tiled=True)

    slim = lax.dynamic_slice(isometry, (0, 0, 0, chan * fine), (1, 2, window, fine))
    slim = slim[0].transpose(0, 2, 1).reshape(2, part, TILE)
    slices = lax.dynamic_slice_in_dim(isometry, chan * part, part, 2)
    kinds = jnp.concatenate([slim[None], slices])
    kinds = kinds.reshape(3, tiles, piece, TILE).transpose(1, 0, 2, 3)
    spread = deliver(kinds.reshape(tiles, 3 * piece, TILE)).reshape(tiles, 3, piece, TILE)

    own, target, anchor = layout_tables(sector_sizes, joining_table, tiles)
    width = pick(own[1], position) * TILE
    anchor_width = pick(anchor[1][0], position) * TILE
    width, anchor_width, spread = lax.optimization_barrier((width, anchor_width, spread))
    mine = sources(*own, tiles).astype(BF16)
    theirs = sources(*target, tiles).astype(BF16)
    theirs = jnp.where(position < half, theirs[:, 0], theirs[:, 1])
    picks = [(theirs[0], 0), (mine, 1), (theirs[1], 2), (mine, 2)]
    routed = [
        jnp.einsum("nit,trd->nird", hot, spread[:, kind], preferred_element_type=F32)
        for hot, kind in picks
    ]
    routed = jnp.stack(routed, axis=1).astype(BF16)
    landed = deliver(routed.reshape(tiles, 4 * MAXK * piece, TILE))
    landed = landed.reshape(2, half, 4, MAXK, piece, TILE)

    def rows_of(groups):
        return groups.transpose(1, 4, 2, 0, 3, 5).reshape(part, -1)

    maps_a = lax.all_gather(rows_of(landed[:, :, 1:3]), "chan", axis=0, tiled=True)
    maps_b = lax.all_gather(rows_of(landed[:, :, 3:4]), "chan", axis=0, tiled=True)
    slim = landed[:, :, 0].transpose(0, 2, 1, 3, 4).reshape(2 * MAXK * fine, window)
    column = jnp.arange(window, dtype=jnp.int32)
    slim = jnp.where(column < width, slim, jnp.zeros((), BF16))

    first = jnp.einsum("dj,waj->wda", slim, gathered, preferred_element_type=F32).astype(BF16)
    first = first.reshape(2, CHANS, 2 * MAXK, fine, TILE).transpose(3, 0, 2, 1, 4)
    first = deliver(first.reshape(tiles, 2 * MAXK * CHANS, TILE))
    select0 = selection(own[0], (anchor[0][0], anchor[1][0]), tiles)
    first = route(select0, first.reshape(tiles, 2, MAXK, CHANS, TILE))
    first = deliver(first.reshape(tiles, 2 * MAXK * CHANS, TILE))
    rows = first.reshape(tiles, 2, MAXK, CHANS, TILE).transpose(1, 0, 3, 2, 4)
    rows = rows.reshape(2, tiles * CHANS, window)

    row = jnp.arange(tiles * CHANS, dtype=jnp.int32)
    channel = jnp.arange(2 * CHANS, dtype=jnp.int32)
    natural = ((row % (2 * CHANS))[:, None] == channel).astype(F32)
    paired = 2 * (row % CHANS) + (row // CHANS) % 2
    paired = (paired[:, None] == channel).astype(F32)
    same = (row // (2 * CHANS))[:, None] == (row // (2 * CHANS))[None, :]

    def blend(coefficients, out_rows):
        spread_out = jnp.einsum("rv,wv->rw", out_rows, coefficients, precision=exact)
        spread_out = jnp.einsum("rw,qw->rq", spread_out, natural, precision=exact)
        return jnp.where(same, spread_out, 0.0)

    scale0 = 3.0 / anchor_width.astype(F32)
    scale1 = 3.0 / width.astype(F32)
    mixed = jnp.zeros((tiles * CHANS, window), F32)
    for s in range(2):
        second = jnp.dot(
            rows[s], maps_a[:, s * window : (s + 1) * window], preferred_element_type=F32
        )
        mixed = mixed + jnp.dot(blend(mixing[0, s] * scale0[s], natural), second, precision=fast)
    middle = mixed.astype(BF16)

    fourth = []
    for s in range(2, 4):
        third = jnp.dot(
            middle, maps_a[:, s * window : (s + 1) * window], preferred_element_type=F32
        )
        fourth.append(jnp.dot(blend(mixing[1, s - 2] * scale1, paired), third, precision=fast))
    fourth = jnp.stack(fourth, axis=1).astype(BF16)
    fourth = lax.all_to_all(fourth, ("sector", "chan"), 0, 0, tiled=True)
    fourth = fourth.reshape(tiles, CHANS, 2, MAXK, TILE).transpose(0, 2, 3, 1, 4)
    select1 = selection(own[0], (anchor[0][1], anchor[1][1]), tiles)
    fourth = deliver(route(select1, fourth).reshape(tiles, 2 * MAXK * CHANS, TILE))
    result = jnp.einsum(
        "jvsicb,icjsd->bvd",
        fourth.reshape(fine, 2, 2, MAXK, CHANS, TILE),
        maps_b.reshape(MAXK, CHANS, fine, 2, window),
        preferred_element_type=F32,
    )
    return result.astype(BF16)


def solution(mesh):
    placed = (P("sector", "chan", None), P(), P(), P(None, None, None, "sector"), P())
    return jax.shard_map(
        per_device, mesh=mesh, in_specs=placed, out_specs=P("sector", "chan", None), check_vma=False
    )
```

```python
import jax
import jax.numpy as jnp
from jax import lax
from jax.sharding import PartitionSpec as P

TILE = 128
NSEC = 16
MAXK = 5
CHANS = 8
BF16 = jnp.bfloat16
F32 = jnp.float32


def pick(table, position):
    ids = jnp.arange(table.shape[-1], dtype=jnp.int32)
    return jnp.sum(jnp.where(ids == position, table, 0), axis=-1)


def layout_tables(sector_sizes, joining_table, tiles):
    counts = sector_sizes // TILE
    ids = jnp.arange(NSEC, dtype=jnp.int32)
    starts = jnp.sum(jnp.where(ids[None, :] < ids[:, None], counts[None, :], 0), axis=1)
    tile = jnp.arange(tiles, dtype=jnp.int32)
    member = (tile[:, None] >= starts[None, :]) & (tile[:, None] < (starts + counts)[None, :])
    joined = joining_table[..., None] == ids

    def by_tile(per_sector):
        return jnp.sum(jnp.where(member, per_sector[..., None, :], 0), axis=-1)

    def both(select):
        return by_tile(select(starts)), by_tile(select(counts))

    own = both(lambda v: v)
    target = both(lambda v: jnp.sum(jnp.where(joined, v, 0), axis=-1))
    anchor = both(lambda v: jnp.sum(jnp.where(joined, v[:, None], 0), axis=-2))
    return own, target, anchor


def sources(start, count, tiles):
    slot = jnp.arange(MAXK, dtype=jnp.int32)
    tile = jnp.arange(tiles, dtype=jnp.int32)
    wanted = jnp.where(slot < count[..., None], start[..., None] + slot, -1)
    return wanted[..., None] == tile


def selection(own_start, anchor, tiles):
    slot = jnp.arange(MAXK, dtype=jnp.int32)
    tile = jnp.arange(tiles, dtype=jnp.int32)
    block = (tile - own_start)[:, None] == slot
    return (sources(*anchor, tiles)[..., None] & block[None, :, None, None, :]).astype(BF16)


def route(chosen, spread):
    return jnp.einsum("snitj,tsjca->nsica", chosen, spread, preferred_element_type=F32).astype(BF16)


def deliver(blocks):
    return lax.all_to_all(blocks, "sector", 0, 0, tiled=True)


def per_device(environment, sector_sizes, joining_table, isometry, mixing):
    tiles = lax.axis_size("sector")
    position = lax.axis_index("sector")
    chan = lax.axis_index("chan")
    window = environment.shape[2]
    part = window // CHANS
    fine = TILE // CHANS
    half = tiles // 2
    piece = part // half
    exact, fast = lax.Precision.HIGHEST, lax.Precision.HIGH

    gathered = lax.all_gather(environment.transpose(1, 0, 2), "chan", axis=0, tiled=True)

    slim = lax.dynamic_slice(isometry, (0, 0, 0, chan * fine), (1, 2, window, fine))
    slim = slim[0].transpose(0, 2, 1).reshape(2, part, TILE)
    slices = lax.dynamic_slice_in_dim(isometry, chan * part, part, 2)
    kinds = jnp.concatenate([slim[None], slices])
    kinds = kinds.reshape(3, tiles, piece, TILE).transpose(1, 0, 2, 3)
    spread = deliver(kinds.reshape(tiles, 3 * piece, TILE)).reshape(tiles, 3, piece, TILE)

    own, target, anchor = layout_tables(sector_sizes, joining_table, tiles)
    width = pick(own[1], position) * TILE
    anchor_width = pick(anchor[1][0], position) * TILE
    width, anchor_width, spread = lax.optimization_barrier((width, anchor_width, spread))
    mine = sources(*own, tiles).astype(BF16)
    theirs = sources(*target, tiles).astype(BF16)
    theirs = jnp.where(position < half, theirs[:, 0], theirs[:, 1])
    picks = [(theirs[0], 0), (mine, 1), (theirs[1], 2), (mine, 2)]
    routed = [
        jnp.einsum("nit,trd->nird", hot, spread[:, kind], preferred_element_type=F32)
        for hot, kind in picks
    ]
    routed = jnp.stack(routed, axis=1).astype(BF16)
    landed = deliver(routed.reshape(tiles, 4 * MAXK * piece, TILE))
    landed = landed.reshape(2, half, 4, MAXK, piece, TILE)

    def rows_of(groups):
        return groups.transpose(1, 4, 2, 0, 3, 5).reshape(part, -1)

    maps_a = lax.all_gather(rows_of(landed[:, :, 1:3]), "chan", axis=0, tiled=True)
    maps_b = lax.all_gather(rows_of(landed[:, :, 3:4]), "chan", axis=0, tiled=True)
    slim = landed[:, :, 0].transpose(0, 2, 1, 3, 4).reshape(2 * MAXK * fine, window)
    column = jnp.arange(window, dtype=jnp.int32)
    slim = jnp.where(column < width, slim, jnp.zeros((), BF16))

    first = jnp.einsum("dj,waj->wda", slim, gathered, preferred_element_type=F32).astype(BF16)
    first = first.reshape(2, CHANS, 2 * MAXK, fine, TILE).transpose(3, 0, 2, 1, 4)
    first = deliver(first.reshape(tiles, 2 * MAXK * CHANS, TILE))
    select0 = selection(own[0], (anchor[0][0], anchor[1][0]), tiles)
    select1 = selection(own[0], (anchor[0][1], anchor[1][1]), tiles)
    first, select1 = lax.optimization_barrier((first, select1))
    first = route(select0, first.reshape(tiles, 2, MAXK, CHANS, TILE))
    first = deliver(first.reshape(tiles, 2 * MAXK * CHANS, TILE))
    rows = first.reshape(tiles, 2, MAXK, CHANS, TILE).transpose(1, 0, 3, 2, 4)
    rows = rows.reshape(2, tiles * CHANS, window)

    row = jnp.arange(tiles * CHANS, dtype=jnp.int32)
    channel = jnp.arange(2 * CHANS, dtype=jnp.int32)
    natural = ((row % (2 * CHANS))[:, None] == channel).astype(F32)
    paired = 2 * (row % CHANS) + (row // CHANS) % 2
    paired = (paired[:, None] == channel).astype(F32)
    same = (row // (2 * CHANS))[:, None] == (row // (2 * CHANS))[None, :]

    def blend(coefficients, out_rows):
        spread_out = jnp.einsum("rv,wv->rw", out_rows, coefficients, precision=exact)
        spread_out = jnp.einsum("rw,qw->rq", spread_out, natural, precision=exact)
        return jnp.where(same, spread_out, 0.0)

    scale0 = 3.0 / anchor_width.astype(F32)
    scale1 = 3.0 / width.astype(F32)
    mixed = jnp.zeros((tiles * CHANS, window), F32)
    for s in range(2):
        second = jnp.dot(
            rows[s], maps_a[:, s * window : (s + 1) * window], preferred_element_type=F32
        )
        mixed = mixed + jnp.dot(blend(mixing[0, s] * scale0[s], natural), second, precision=fast)
    middle = mixed.astype(BF16)

    fourth = []
    for s in range(2, 4):
        third = jnp.dot(
            middle, maps_a[:, s * window : (s + 1) * window], preferred_element_type=F32
        )
        fourth.append(jnp.dot(blend(mixing[1, s - 2] * scale1, paired), third, precision=fast))
    fourth = jnp.stack(fourth, axis=1).astype(BF16)
    fourth = lax.all_to_all(fourth, ("sector", "chan"), 0, 0, tiled=True)
    fourth = fourth.reshape(tiles, CHANS, 2, MAXK, TILE).transpose(0, 2, 3, 1, 4)
    fourth = deliver(route(select1, fourth).reshape(tiles, 2 * MAXK * CHANS, TILE))
    result = jnp.einsum(
        "jvsicb,icjsd->bvd",
        fourth.reshape(fine, 2, 2, MAXK, CHANS, TILE),
        maps_b.reshape(MAXK, CHANS, fine, 2, window),
        preferred_element_type=F32,
    )
    return result.astype(BF16)


def solution(mesh):
    placed = (P("sector", "chan", None), P(), P(), P(None, None, None, "sector"), P())
    return jax.shard_map(
        per_device, mesh=mesh, in_specs=placed, out_specs=P("sector", "chan", None), check_vma=False
    )
```

```python
import jax
import jax.numpy as jnp
from jax import lax
from jax.sharding import PartitionSpec as P


TILE = 128
NSEC = 16
MAXK = 5
CHANS = 8
BF16 = jnp.bfloat16
F32 = jnp.float32


def pick(table, position):
    ids = jnp.arange(table.shape[-1], dtype=jnp.int32)
    return jnp.sum(jnp.where(ids == position, table, 0), axis=-1)


def layout_tables(sector_sizes, joining_table, tiles):
    counts = sector_sizes // TILE
    ids = jnp.arange(NSEC, dtype=jnp.int32)
    starts = jnp.sum(jnp.where(ids[None, :] < ids[:, None], counts[None, :], 0), axis=1)
    tile = jnp.arange(tiles, dtype=jnp.int32)
    member = (tile[:, None] >= starts[None, :]) & (tile[:, None] < (starts + counts)[None, :])
    joined = joining_table[..., None] == ids

    def by_tile(per_sector):
        return jnp.sum(jnp.where(member, per_sector[..., None, :], 0), axis=-1)

    def both(select):
        return by_tile(select(starts)), by_tile(select(counts))

    own = both(lambda v: v)
    target = both(lambda v: jnp.sum(jnp.where(joined, v, 0), axis=-1))
    anchor = both(lambda v: jnp.sum(jnp.where(joined, v[:, None], 0), axis=-2))
    return own, target, anchor


def sources(start, count, tiles):
    slot = jnp.arange(MAXK, dtype=jnp.int32)
    tile = jnp.arange(tiles, dtype=jnp.int32)
    wanted = jnp.where(slot < count[..., None], start[..., None] + slot, -1)
    return wanted[..., None] == tile


def selection(own_start, anchor, tiles):
    slot = jnp.arange(MAXK, dtype=jnp.int32)
    tile = jnp.arange(tiles, dtype=jnp.int32)
    block = (tile - own_start)[:, None] == slot
    return (sources(*anchor, tiles)[..., None] & block[None, :, None, None, :]).astype(BF16)


def route(chosen, spread):
    return jnp.einsum("snitj,tsjca->nsica", chosen, spread, preferred_element_type=F32).astype(BF16)


def deliver(blocks):
    return lax.all_to_all(blocks, "sector", 0, 0, tiled=True)


def per_device(environment, sector_sizes, joining_table, isometry, mixing):
    tiles = lax.axis_size("sector")
    position = lax.axis_index("sector")
    chan = lax.axis_index("chan")
    window = environment.shape[2]
    part = window // CHANS
    fine = TILE // CHANS
    half = tiles // 2
    piece = part // half
    exact, fast = lax.Precision.HIGHEST, lax.Precision.HIGH

    gathered = lax.all_gather(environment.transpose(1, 0, 2), "chan", axis=0, tiled=True)

    slim = lax.dynamic_slice(isometry, (0, 0, 0, chan * fine), (1, 2, window, fine))
    slim = slim[0].transpose(0, 2, 1).reshape(2, part, TILE)
    slices = lax.dynamic_slice_in_dim(isometry, chan * part, part, 2)
    kinds = jnp.concatenate([slim[None], slices])
    kinds = kinds.reshape(3, tiles, piece, TILE).transpose(1, 0, 2, 3)
    spread = deliver(kinds.reshape(tiles, 3 * piece, TILE)).reshape(tiles, 3, piece, TILE)

    own, target, anchor = layout_tables(sector_sizes, joining_table, tiles)
    width = pick(own[1], position) * TILE
    anchor_width = pick(anchor[1][0], position) * TILE
    width, anchor_width, spread = lax.optimization_barrier((width, anchor_width, spread))
    mine = sources(*own, tiles).astype(BF16)
    theirs = sources(*target, tiles).astype(BF16)
    theirs = jnp.where(position < half, theirs[:, 0], theirs[:, 1])
    picks = [(theirs[0], 0), (mine, 1), (theirs[1], 2), (mine, 2)]
    routed = [
        jnp.einsum("nit,trd->nird", hot, spread[:, kind], preferred_element_type=F32)
        for hot, kind in picks
    ]
    routed = jnp.stack(routed, axis=1).astype(BF16)
    landed = deliver(routed.reshape(tiles, 4 * MAXK * piece, TILE))
    landed = landed.reshape(2, half, 4, MAXK, piece, TILE)

    def rows_of(groups):
        return groups.transpose(1, 4, 2, 0, 3, 5).reshape(part, -1)

    laid = rows_of(landed[:, :, 1:3])
    maps_a = lax.all_gather(laid, "chan", axis=0, tiled=True)
    maps_b = lax.all_gather(rows_of(landed[:, :, 3:4]), "chan", axis=0, tiled=True)
    slim = landed[:, :, 0].transpose(0, 2, 1, 3, 4).reshape(2 * MAXK * fine, window)
    column = jnp.arange(window, dtype=jnp.int32)
    slim = jnp.where(column < width, slim, jnp.zeros((), BF16))

    first = jnp.einsum("dj,waj->wda", slim, gathered, preferred_element_type=F32).astype(BF16)
    first = first.reshape(2, CHANS, 2 * MAXK, fine, TILE).transpose(3, 0, 2, 1, 4)
    first = first.reshape(tiles, 2 * MAXK * CHANS, TILE)
    first = deliver(first)
    select0 = selection(own[0], (anchor[0][0], anchor[1][0]), tiles)
    select1 = selection(own[0], (anchor[0][1], anchor[1][1]), tiles)
    first, select1 = lax.optimization_barrier((first, select1))
    first = route(select0, first.reshape(tiles, 2, MAXK, CHANS, TILE))
    first = deliver(first.reshape(tiles, 2 * MAXK * CHANS, TILE))
    rows = first.reshape(tiles, 2, MAXK, CHANS, TILE).transpose(1, 0, 3, 2, 4)
    rows = rows.reshape(2, tiles * CHANS, window)

    row = jnp.arange(tiles * CHANS, dtype=jnp.int32)
    channel = jnp.arange(2 * CHANS, dtype=jnp.int32)
    natural = ((row % (2 * CHANS))[:, None] == channel).astype(F32)
    paired = 2 * (row % CHANS) + (row // CHANS) % 2
    paired = (paired[:, None] == channel).astype(F32)
    same = (row // (2 * CHANS))[:, None] == (row // (2 * CHANS))[None, :]

    def blend(coefficients, out_rows):
        spread_out = jnp.einsum("rv,wv->rw", out_rows, coefficients, precision=exact)
        spread_out = jnp.einsum("rw,qw->rq", spread_out, natural, precision=exact)
        return jnp.where(same, spread_out, 0.0)

    scale0 = 3.0 / anchor_width.astype(F32)
    scale1 = 3.0 / width.astype(F32)
    mixed = jnp.zeros((tiles * CHANS, window), F32)
    for s in range(2):
        second = jnp.dot(
            rows[s], maps_a[:, s * window : (s + 1) * window], preferred_element_type=F32
        )
        mixed = mixed + jnp.dot(blend(mixing[0, s] * scale0[s], natural), second, precision=fast)
    middle = mixed.astype(BF16)

    fourth = []
    for s in range(2, 4):
        third = jnp.dot(
            middle, maps_a[:, s * window : (s + 1) * window], preferred_element_type=F32
        )
        fourth.append(jnp.dot(blend(mixing[1, s - 2] * scale1, paired), third, precision=fast))
    fourth = jnp.stack(fourth, axis=1).astype(BF16)
    fourth = lax.all_to_all(fourth, ("sector", "chan"), 0, 0, tiled=True)
    fourth = fourth.reshape(tiles, CHANS, 2, MAXK, TILE).transpose(0, 2, 3, 1, 4)
    fourth = deliver(route(select1, fourth).reshape(tiles, 2 * MAXK * CHANS, TILE))
    result = jnp.einsum(
        "jvsicb,icjsd->bvd",
        fourth.reshape(fine, 2, 2, MAXK, CHANS, TILE),
        maps_b.reshape(MAXK, CHANS, fine, 2, window),
        preferred_element_type=F32,
    )
    return result.astype(BF16)


def solution(mesh):
    placed = (P("sector", "chan", None), P(), P(), P(None, None, None, "sector"), P())
    return jax.shard_map(
        per_device, mesh=mesh, in_specs=placed, out_specs=P("sector", "chan", None), check_vma=False
    )
```

```python
import jax
import jax.numpy as jnp
from jax import lax
from jax.sharding import PartitionSpec as P


TILE = 128
NSEC = 16
MAXK = 5
CHANS = 8
BF16 = jnp.bfloat16
F32 = jnp.float32


def pick(table, position):
    ids = jnp.arange(table.shape[-1], dtype=jnp.int32)
    return jnp.sum(jnp.where(ids == position, table, 0), axis=-1)


def layout_tables(sector_sizes, joining_table, tiles):
    counts = sector_sizes // TILE
    ids = jnp.arange(NSEC, dtype=jnp.int32)
    starts = jnp.sum(jnp.where(ids[None, :] < ids[:, None], counts[None, :], 0), axis=1)
    tile = jnp.arange(tiles, dtype=jnp.int32)
    member = (tile[:, None] >= starts[None, :]) & (tile[:, None] < (starts + counts)[None, :])
    joined = joining_table[..., None] == ids

    def by_tile(per_sector):
        return jnp.sum(jnp.where(member, per_sector[..., None, :], 0), axis=-1)

    def both(select):
        return by_tile(select(starts)), by_tile(select(counts))

    own = both(lambda v: v)
    target = both(lambda v: jnp.sum(jnp.where(joined, v, 0), axis=-1))
    anchor = both(lambda v: jnp.sum(jnp.where(joined, v[:, None], 0), axis=-2))
    return own, target, anchor


def sources(start, count, tiles):
    slot = jnp.arange(MAXK, dtype=jnp.int32)
    tile = jnp.arange(tiles, dtype=jnp.int32)
    wanted = jnp.where(slot < count[..., None], start[..., None] + slot, -1)
    return wanted[..., None] == tile


def selection(own_start, anchor, tiles):
    slot = jnp.arange(MAXK, dtype=jnp.int32)
    tile = jnp.arange(tiles, dtype=jnp.int32)
    block = (tile - own_start)[:, None] == slot
    return (sources(*anchor, tiles)[..., None] & block[None, :, None, None, :]).astype(BF16)


def route(chosen, spread):
    return jnp.einsum("snitj,tsjca->nsica", chosen, spread, preferred_element_type=F32).astype(BF16)


def deliver(blocks):
    return lax.all_to_all(blocks, "sector", 0, 0, tiled=True)


def per_device(environment, sector_sizes, joining_table, isometry, mixing):
    tiles = lax.axis_size("sector")
    position = lax.axis_index("sector")
    chan = lax.axis_index("chan")
    window = environment.shape[2]
    part = window // CHANS
    fine = TILE // CHANS
    half = tiles // 2
    piece = part // half
    exact, fast = lax.Precision.HIGHEST, lax.Precision.HIGH

    gathered = lax.all_gather(environment.transpose(1, 0, 2), "chan", axis=0, tiled=True)

    slim = lax.dynamic_slice(isometry, (0, 0, 0, chan * fine), (1, 2, window, fine))
    slim = slim[0].transpose(0, 2, 1).reshape(2, part, TILE)
    slices = lax.dynamic_slice_in_dim(isometry, chan * part, part, 2)
    kinds = jnp.concatenate([slim[None], slices])
    kinds = kinds.reshape(3, tiles, piece, TILE).transpose(1, 0, 2, 3)
    spread = deliver(kinds.reshape(tiles, 3 * piece, TILE)).reshape(tiles, 3, piece, TILE)

    own, target, anchor = layout_tables(sector_sizes, joining_table, tiles)
    width = pick(own[1], position) * TILE
    anchor_width = pick(anchor[1][0], position) * TILE
    width, anchor_width, spread = lax.optimization_barrier((width, anchor_width, spread))
    mine = sources(*own, tiles).astype(BF16)
    theirs = sources(*target, tiles).astype(BF16)
    theirs = jnp.where(position < half, theirs[:, 0], theirs[:, 1])
    picks = [(theirs[0], 0), (mine, 1), (theirs[1], 2), (mine, 2)]
    routed = [
        jnp.einsum("nit,trd->nird", hot, spread[:, kind], preferred_element_type=F32)
        for hot, kind in picks
    ]
    routed = jnp.stack(routed, axis=1).astype(BF16)
    landed = deliver(routed.reshape(tiles, 4 * MAXK * piece, TILE))
    landed = landed.reshape(2, half, 4, MAXK, piece, TILE)

    landed, width, own_start, anchor = lax.optimization_barrier((landed, width, own[0], anchor))

    def rows_of(groups):
        return groups.transpose(1, 4, 2, 0, 3, 5).reshape(part, -1)

    laid = rows_of(landed[:, :, 1:3])
    maps_a = lax.all_gather(laid, "chan", axis=0, tiled=True)
    maps_b = lax.all_gather(rows_of(landed[:, :, 3:4]), "chan", axis=0, tiled=True)
    slim = landed[:, :, 0].transpose(0, 2, 1, 3, 4).reshape(2 * MAXK * fine, window)
    column = jnp.arange(window, dtype=jnp.int32)
    slim = jnp.where(column < width, slim, jnp.zeros((), BF16))

    first = jnp.einsum("dj,waj->wda", slim, gathered, preferred_element_type=F32).astype(BF16)
    first = first.reshape(2, CHANS, 2 * MAXK, fine, TILE).transpose(3, 0, 2, 1, 4)
    first = first.reshape(tiles, 2 * MAXK * CHANS, TILE)
    first = deliver(first)
    select0 = selection(own_start, (anchor[0][0], anchor[1][0]), tiles)
    select1 = selection(own_start, (anchor[0][1], anchor[1][1]), tiles)
    first, select1 = lax.optimization_barrier((first, select1))
    first = route(select0, first.reshape(tiles, 2, MAXK, CHANS, TILE))
    first = deliver(first.reshape(tiles, 2 * MAXK * CHANS, TILE))
    rows = first.reshape(tiles, 2, MAXK, CHANS, TILE).transpose(1, 0, 3, 2, 4)
    rows = rows.reshape(2, tiles * CHANS, window)

    row = jnp.arange(tiles * CHANS, dtype=jnp.int32)
    channel = jnp.arange(2 * CHANS, dtype=jnp.int32)
    natural = ((row % (2 * CHANS))[:, None] == channel).astype(F32)
    paired = 2 * (row % CHANS) + (row // CHANS) % 2
    paired = (paired[:, None] == channel).astype(F32)
    same = (row // (2 * CHANS))[:, None] == (row // (2 * CHANS))[None, :]

    def blend(coefficients, out_rows):
        spread_out = jnp.einsum("rv,wv->rw", out_rows, coefficients, precision=exact)
        spread_out = jnp.einsum("rw,qw->rq", spread_out, natural, precision=exact)
        return jnp.where(same, spread_out, 0.0)

    scale0 = 3.0 / anchor_width.astype(F32)
    scale1 = 3.0 / width.astype(F32)
    mixed = jnp.zeros((tiles * CHANS, window), F32)
    for s in range(2):
        second = jnp.dot(
            rows[s], maps_a[:, s * window : (s + 1) * window], preferred_element_type=F32
        )
        mixed = mixed + jnp.dot(blend(mixing[0, s] * scale0[s], natural), second, precision=fast)
    middle = mixed.astype(BF16)

    fourth = []
    for s in range(2, 4):
        third = jnp.dot(
            middle, maps_a[:, s * window : (s + 1) * window], preferred_element_type=F32
        )
        fourth.append(jnp.dot(blend(mixing[1, s - 2] * scale1, paired), third, precision=fast))
    fourth = jnp.stack(fourth, axis=1).astype(BF16)
    fourth = lax.all_to_all(fourth, ("sector", "chan"), 0, 0, tiled=True)
    fourth = fourth.reshape(tiles, CHANS, 2, MAXK, TILE).transpose(0, 2, 3, 1, 4)
    fourth = deliver(route(select1, fourth).reshape(tiles, 2 * MAXK * CHANS, TILE))
    result = jnp.einsum(
        "jvsicb,icjsd->bvd",
        fourth.reshape(fine, 2, 2, MAXK, CHANS, TILE),
        maps_b.reshape(MAXK, CHANS, fine, 2, window),
        preferred_element_type=F32,
    )
    return result.astype(BF16)


def solution(mesh):
    placed = (P("sector", "chan", None), P(), P(), P(None, None, None, "sector"), P())
    return jax.shard_map(
        per_device, mesh=mesh, in_specs=placed, out_specs=P("sector", "chan", None), check_vma=False
    )
```

```python
import jax
import jax.numpy as jnp
from jax import lax
from jax.sharding import PartitionSpec as P


TILE = 128
NSEC = 16
MAXK = 5
CHANS = 8
BF16 = jnp.bfloat16
F32 = jnp.float32


def pick(table, position):
    ids = jnp.arange(table.shape[-1], dtype=jnp.int32)
    return jnp.sum(jnp.where(ids == position, table, 0), axis=-1)


def layout_tables(sector_sizes, joining_table, tiles):
    counts = sector_sizes // TILE
    ids = jnp.arange(NSEC, dtype=jnp.int32)
    starts = jnp.sum(jnp.where(ids[None, :] < ids[:, None], counts[None, :], 0), axis=1)
    tile = jnp.arange(tiles, dtype=jnp.int32)
    member = (tile[:, None] >= starts[None, :]) & (tile[:, None] < (starts + counts)[None, :])
    joined = joining_table[..., None] == ids

    def by_tile(per_sector):
        return jnp.sum(jnp.where(member, per_sector[..., None, :], 0), axis=-1)

    def both(select):
        return by_tile(select(starts)), by_tile(select(counts))

    own = both(lambda v: v)
    target = both(lambda v: jnp.sum(jnp.where(joined, v, 0), axis=-1))
    anchor = both(lambda v: jnp.sum(jnp.where(joined, v[:, None], 0), axis=-2))
    return own, target, anchor


def sources(start, count, tiles):
    slot = jnp.arange(MAXK, dtype=jnp.int32)
    tile = jnp.arange(tiles, dtype=jnp.int32)
    wanted = jnp.where(slot < count[..., None], start[..., None] + slot, -1)
    return wanted[..., None] == tile


def selection(own_start, anchor, tiles):
    slot = jnp.arange(MAXK, dtype=jnp.int32)
    tile = jnp.arange(tiles, dtype=jnp.int32)
    block = (tile - own_start)[:, None] == slot
    return (sources(*anchor, tiles)[..., None] & block[None, :, None, None, :]).astype(BF16)


def route(chosen, spread):
    return jnp.einsum("snitj,tsjca->nsica", chosen, spread, preferred_element_type=F32).astype(BF16)


def deliver(blocks):
    return lax.all_to_all(blocks, "sector", 0, 0, tiled=True)


def per_device(environment, sector_sizes, joining_table, isometry, mixing):
    tiles = lax.axis_size("sector")
    position = lax.axis_index("sector")
    chan = lax.axis_index("chan")
    window = environment.shape[2]
    part = window // CHANS
    fine = TILE // CHANS
    half = tiles // 2
    piece = part // half
    exact, fast = lax.Precision.HIGHEST, lax.Precision.HIGH

    gathered = lax.all_gather(environment.transpose(1, 0, 2), "chan", axis=0, tiled=True)

    slim = lax.dynamic_slice(isometry, (0, 0, 0, chan * fine), (1, 2, window, fine))
    slim = slim[0].transpose(0, 2, 1).reshape(2, part, TILE)
    slices = lax.dynamic_slice_in_dim(isometry, chan * part, part, 2)
    kinds = jnp.concatenate([slim[None], slices])
    kinds = kinds.reshape(3, tiles, piece, TILE).transpose(1, 0, 2, 3)
    spread = deliver(kinds.reshape(tiles, 3 * piece, TILE)).reshape(tiles, 3, piece, TILE)

    own, target, anchor = layout_tables(sector_sizes, joining_table, tiles)
    width = pick(own[1], position) * TILE
    anchor_width = pick(anchor[1][0], position) * TILE
    width, anchor_width, spread = lax.optimization_barrier((width, anchor_width, spread))
    mine = sources(*own, tiles).astype(BF16)
    theirs = sources(*target, tiles).astype(BF16)
    theirs = jnp.where(position < half, theirs[:, 0], theirs[:, 1])
    picks = [(theirs[0], 0), (mine, 1), (theirs[1], 2), (mine, 2)]
    routed = [
        jnp.einsum("nit,trd->nird", hot, spread[:, kind], preferred_element_type=F32)
        for hot, kind in picks
    ]
    routed = jnp.stack(routed, axis=1).astype(BF16)
    landed = deliver(routed.reshape(tiles, 4 * MAXK * piece, TILE))
    landed = landed.reshape(2, half, 4, MAXK, piece, TILE)

    landed, width, own_start, anchor = lax.optimization_barrier((landed, width, own[0], anchor))

    def rows_of(groups):
        return groups.transpose(1, 4, 2, 0, 3, 5).reshape(part, -1)

    laid = rows_of(landed[:, :, 1:3])
    maps_a = lax.all_gather(laid, "chan", axis=0, tiled=True)
    laid = rows_of(landed[:, :, 3:4])
    maps_b = lax.all_gather(laid, "chan", axis=0, tiled=True)
    slim = landed[:, :, 0].transpose(0, 2, 1, 3, 4).reshape(2 * MAXK * fine, window)
    column = jnp.arange(window, dtype=jnp.int32)
    slim = jnp.where(column < width, slim, jnp.zeros((), BF16))

    first = jnp.einsum("dj,waj->wda", slim, gathered, preferred_element_type=F32).astype(BF16)
    first = first.reshape(2, CHANS, 2 * MAXK, fine, TILE).transpose(3, 0, 2, 1, 4)
    first = first.reshape(tiles, 2 * MAXK * CHANS, TILE)
    first = deliver(first)
    select0 = selection(own_start, (anchor[0][0], anchor[1][0]), tiles)
    select1 = selection(own_start, (anchor[0][1], anchor[1][1]), tiles)
    first, select1 = lax.optimization_barrier((first, select1))
    first = route(select0, first.reshape(tiles, 2, MAXK, CHANS, TILE))
    first = deliver(first.reshape(tiles, 2 * MAXK * CHANS, TILE))
    rows = first.reshape(tiles, 2, MAXK, CHANS, TILE).transpose(1, 0, 3, 2, 4)
    rows = rows.reshape(2, tiles * CHANS, window)

    row = jnp.arange(tiles * CHANS, dtype=jnp.int32)
    channel = jnp.arange(2 * CHANS, dtype=jnp.int32)
    natural = ((row % (2 * CHANS))[:, None] == channel).astype(F32)
    paired = 2 * (row % CHANS) + (row // CHANS) % 2
    paired = (paired[:, None] == channel).astype(F32)
    same = (row // (2 * CHANS))[:, None] == (row // (2 * CHANS))[None, :]

    def blend(coefficients, out_rows):
        spread_out = jnp.einsum("rv,wv->rw", out_rows, coefficients, precision=exact)
        spread_out = jnp.einsum("rw,qw->rq", spread_out, natural, precision=exact)
        return jnp.where(same, spread_out, 0.0)

    scale0 = 3.0 / anchor_width.astype(F32)
    scale1 = 3.0 / width.astype(F32)
    blends = [blend(mixing[0, s] * scale0[s], natural) for s in range(2)]
    blends += [blend(mixing[1, s] * scale1, paired) for s in range(2)]
    mixed = jnp.zeros((tiles * CHANS, window), F32)
    for s in range(2):
        second = jnp.dot(
            rows[s], maps_a[:, s * window : (s + 1) * window], preferred_element_type=F32
        )
        mixed = mixed + jnp.dot(blends[s], second, precision=fast)
    middle = mixed.astype(BF16)

    fourth = []
    for s in range(2, 4):
        third = jnp.dot(
            middle, maps_a[:, s * window : (s + 1) * window], preferred_element_type=F32
        )
        fourth.append(jnp.dot(blends[s], third, precision=fast))
    fourth = jnp.stack(fourth, axis=1).astype(BF16)
    fourth = lax.all_to_all(fourth, ("sector", "chan"), 0, 0, tiled=True)
    fourth = fourth.reshape(tiles, CHANS, 2, MAXK, TILE).transpose(0, 2, 3, 1, 4)
    fourth = deliver(route(select1, fourth).reshape(tiles, 2 * MAXK * CHANS, TILE))
    result = jnp.einsum(
        "jvsicb,icjsd->bvd",
        fourth.reshape(fine, 2, 2, MAXK, CHANS, TILE),
        maps_b.reshape(MAXK, CHANS, fine, 2, window),
        preferred_element_type=F32,
    )
    return result.astype(BF16)


def solution(mesh):
    placed = (P("sector", "chan", None), P(), P(), P(None, None, None, "sector"), P())
    return jax.shard_map(
        per_device, mesh=mesh, in_specs=placed, out_specs=P("sector", "chan", None), check_vma=False
    )
```
